128 devices in a mesh: ctx: 32 (over z_lo, y, x), dp: 4 (over z_hi, core).
Axes of the slice: x: 4, y: 4, z: 4 (z_hi: 2, z_lo: 2; z = z_hi * 2 + z_lo), core: 2. Of those that a mesh axis runs over, the one named last changes fastest.
Arguments:
- tokens: bfloat16 [4, 12288, 4096], P('dp', 'ctx'), may hold values from -6 to 6
- key_input: bfloat16 [4, 12288, 2048], P('dp', 'ctx'), may hold values from -6 to 6
- values: bfloat16 [4, 12288, 2048], P('dp', 'ctx'), may hold values from -6 to 6
- q_weight: bfloat16 [4096, 2048], P(('ctx', 'dp')), may hold values from -0.09375 to 0.09375
- q_spikes: int32 [4, 12288, 2048], P('dp', 'ctx'), may hold values 0 or 1
- k_spikes: int32 [4, 12288, 2048], P('dp', 'ctx'), may hold values 0 or 1
- cotangent: bfloat16 [4, 12288, 2048], P('dp', 'ctx'), may hold values from -6 to 6
Outputs:
- attended: bfloat16 [4, 12288, 2048], P('dp', 'ctx')
- grad_tokens: bfloat16 [4, 12288, 4096], P('dp', 'ctx')
- grad_keys: bfloat16 [4, 12288, 2048], P('dp', 'ctx')
- grad_values: bfloat16 [4, 12288, 2048], P('dp', 'ctx')
The draws below stay inside these ranges and needn't reach their ends.
All inputs are finite; a program needn't handle non-finite values. No bound on the sum of `q_spikes` or of `k_spikes` on one device may be relied on, other than what follows from the above.
Results may differ from the reference program's by a relative error of at most 0.005.
Values may be sent and summed in bfloat16 or wider, within the bound.
A program may use at most 256 MiB of HBM per device.

```python
import math
import jax
import jax.numpy as jnp
from jax import lax

D = 4096
HEADS = 16
HEAD = 128
TOK_DEV = 384
HD = 2048
SEQ = 12288
BATCH = 4
N_CTX = 32


def with_ends(drawn, rng, low, high):
    longest = drawn.shape.index(max(drawn.shape))
    spots = []
    for shift in (0, 1):
        where = [jax.random.randint(jax.random.fold_in(rng, axis), (), 0, length) for axis, length in enumerate(drawn.shape)]
        where[longest] = (where[longest] + shift) % drawn.shape[longest]
        spots.append(tuple(where))
    return drawn.at[spots[0]].set(low).at[spots[1]].set(high)


def level_of(rng, dims, split, low, high):
    level = 1.0
    for axis_at, shards_of in split:
        draws = jax.random.uniform(jax.random.fold_in(jax.random.fold_in(rng, 6), axis_at), (shards_of,), jnp.float32, low / len(split), high / len(split))
        level = level * jnp.repeat(jnp.exp(draws), dims[axis_at] // shards_of).reshape((-1,) + (1,) * (len(dims) - 1 - axis_at))
    return level


def gaussian(stream_key, shape, scale, limit, split=(), dtype=jnp.bfloat16):
    values = jax.random.normal(stream_key, shape, jnp.float32) * scale
    if len(split) > 0:
        values = level_of(stream_key, shape, split, -0.22, 0.18) * values
    return jnp.clip(values, min=-limit, max=limit).astype(dtype)


def setup_inputs(seed: int = 0) -> dict:
    seeds = jax.random.split(jax.random.key(seed), 8)
    tokens = gaussian(seeds[0], (BATCH, SEQ, D), 1.0, 6.0, ((0, 4), (1, 32)))
    key_input = gaussian(seeds[1], (BATCH, SEQ, HD), 1.0, 6.0, ((0, 4), (1, 32)))
    values = gaussian(seeds[2], (BATCH, SEQ, HD), 1.0, 6.0, ((0, 4), (1, 32)))
    q_weight = gaussian(seeds[3], (D, HD), D ** -0.5, 0.09375, ((0, 128),))
    q_spikes = with_ends((jax.random.randint(seeds[4], (BATCH, SEQ, HD), 0, 3) < 1).astype(jnp.int32), jax.random.fold_in(seeds[4], 1), 0, 1)
    k_spikes = with_ends((jax.random.randint(seeds[5], (BATCH, SEQ, HD), 0, 3) < 1).astype(jnp.int32), jax.random.fold_in(seeds[5], 1), 0, 1)
    cotangent = gaussian(seeds[6], (BATCH, SEQ, HD), 1.0, 6.0, ((0, 4), (1, 32)))
    return {"tokens": tokens, "key_input": key_input, "values": values, "q_weight": q_weight, "q_spikes": q_spikes, "k_spikes": k_spikes, "cotangent": cotangent}


exact_mode = lax.Precision.HIGHEST

def to_blocks(array):
    shaped = array.astype(jnp.float32).reshape(BATCH, N_CTX, TOK_DEV, HEADS, HEAD)
    return jnp.transpose(shaped, (1, 0, 2, 3, 4))

def from_blocks(array):
    return jnp.transpose(array, (1, 0, 2, 3, 4)).reshape(BATCH, SEQ, HEADS * HEAD)

def rounded(array):
    narrow = lax.optimization_barrier(array.astype(jnp.bfloat16))
    return narrow.astype(jnp.float32)

def reference(tokens, key_input, values, q_weight, q_spikes, k_spikes, cotangent):
    factor = 3.0 / math.sqrt(HEAD * SEQ)
    token_rows = tokens.reshape(BATCH * SEQ, D)
    projected = jnp.dot(token_rows, q_weight, preferred_element_type=jnp.float32).reshape(BATCH, SEQ, HD)
    queries = (projected * q_spikes.astype(jnp.float32)).astype(jnp.bfloat16)
    keys = key_input * k_spikes.astype(jnp.bfloat16)
    block_data = (to_blocks(queries), to_blocks(keys), to_blocks(values), to_blocks(cotangent))
    causal = jnp.tril(jnp.ones((TOK_DEV, TOK_DEV), jnp.float32))

    def both_scores(query_wide, key_wide, value_wide, grad_wide):
        scores = jnp.einsum('blhe,bmhe->bhlm', query_wide, key_wide, precision=exact_mode) * causal
        grad_scores = jnp.einsum('blhf,bmhf->bhlm', grad_wide, value_wide, precision=exact_mode) * causal
        return (rounded(scores), rounded(grad_scores))

    def forward_step(memory, inputs_now):
        query_wide, key_wide, value_wide, grad_wide = inputs_now
        scores, grad_scores = both_scores(query_wide, key_wide, value_wide, grad_wide)
        output = jnp.einsum('bhlm,bmhf->blhf', scores, value_wide, precision=exact_mode)
        output = output + jnp.einsum('blhe,bhef->blhf', query_wide, memory, precision=exact_mode)
        query_grad = jnp.einsum('bhlm,bmhe->blhe', grad_scores, key_wide, precision=exact_mode)
        query_grad = query_grad + jnp.einsum('blhf,bhef->blhe', grad_wide, memory, precision=exact_mode)
        memory = memory + jnp.einsum('blhe,blhf->bhef', key_wide, value_wide, precision=exact_mode)
        return (memory, (output, query_grad))

    def backward_step(memory, inputs_now):
        query_wide, key_wide, value_wide, grad_wide = inputs_now
        scores, grad_scores = both_scores(query_wide, key_wide, value_wide, grad_wide)
        key_grad = jnp.einsum('bhlm,blhe->bmhe', grad_scores, query_wide, precision=exact_mode)
        key_grad = key_grad + jnp.einsum('bmhf,bhef->bmhe', value_wide, memory, precision=exact_mode)
        value_grad = jnp.einsum('bhlm,blhf->bmhf', scores, grad_wide, precision=exact_mode)
        value_grad = value_grad + jnp.einsum('bmhe,bhef->bmhf', key_wide, memory, precision=exact_mode)
        memory = memory + jnp.einsum('blhe,blhf->bhef', query_wide, grad_wide, precision=exact_mode)
        return (memory, (key_grad, value_grad))
    zeroes = jnp.zeros((BATCH, HEADS, HEAD, HEAD), jnp.float32)
    _, (output, query_grad) = lax.scan(forward_step, zeroes, block_data)
    _, (key_grad, value_grad) = lax.scan(backward_step, zeroes, block_data, reverse=True)
    attended = (factor * from_blocks(output)).astype(jnp.bfloat16)
    masked_grad = (factor * from_blocks(query_grad) * q_spikes.astype(jnp.float32)).astype(jnp.bfloat16)
    grad_tokens = jnp.dot(masked_grad.reshape(BATCH * SEQ, HD), q_weight.T, preferred_element_type=jnp.float32)
    grad_tokens = grad_tokens.reshape(BATCH, SEQ, D).astype(jnp.bfloat16)
    grad_keys = (factor * from_blocks(key_grad) * k_spikes.astype(jnp.float32)).astype(jnp.bfloat16)
    grad_values = (factor * from_blocks(value_grad)).astype(jnp.bfloat16)
    return (attended, grad_tokens, grad_keys, grad_values)
```

```python
import functools
import math

import jax
import jax.numpy as jnp
from jax import lax
from jax.experimental import pallas as pl
from jax.experimental.pallas import tpu as pltpu
from jax.sharding import PartitionSpec as P

HEADS = 16
HEAD = 128
GROUPS = 8
GCOLS = 256
N_CTX = 32
PIECE = HEADS * HEAD // N_CTX
MESH = pl.DeviceIdType.MESH
ORDERS = ((0, 1, 2), (1, 2, 0), (2, 0, 1))


def place():
    ctx = lax.axis_index("ctx")
    dp = lax.axis_index("dp")
    x = lax.rem(ctx, 4)
    y = lax.rem(ctx // 4, 4)
    z = (dp // 2) * 2 + ctx // 16
    return (x, y, z), lax.rem(dp, 2)


def device_of(at, core):
    x, y, z = at
    return (lax.rem(z, 2) * 16 + y * 4 + x, (z // 2) * 2 + core)


def moved(at, axis, by):
    out = list(at)
    out[axis] = lax.rem(out[axis] + by, 4)
    return tuple(out)


def view(buf, group, at, core, whole):
    def pick(axis):
        return slice(None) if axis in whole else None

    x, y, z = at
    sx = slice(None) if 0 in whole else x
    sy = slice(None) if 1 in whole else y
    slo = slice(None) if 2 in whole else lax.rem(z, 2)
    shi = slice(None) if 2 in whole else z // 2
    return buf.at[group, slo, sy, sx, shi, core]


def gather_kernel(w_ref, out_ref, own_sem, send_sem, recv_sem, sib_sems):
    at, core = place()
    buf = out_ref
    barrier = pltpu.get_barrier_semaphore()
    for axis in range(3):
        for by in (1, 2, 3):
            pl.semaphore_signal(
                barrier, 1, device_id=device_of(moved(at, axis, by), core), device_id_type=MESH
            )
    pl.semaphore_signal(barrier, 1, device_id=device_of(at, 1 - core), device_id_type=MESH)
    own = []
    for g in range(GROUPS):
        copy = pltpu.make_async_copy(
            w_ref.at[:, pl.ds(g * GCOLS, GCOLS)], view(buf, g, at, core, ()), own_sem.at[g]
        )
        copy.start()
        own.append(copy)
    pl.semaphore_wait(barrier, 10)

    def phase(g, number):
        order = ORDERS[g % 3]
        whole = order[:number]
        part = view(buf, g, at, core, whole)
        copies = []
        for by in (1, 3, 2):
            copy = pltpu.make_async_remote_copy(
                src_ref=part,
                dst_ref=part,
                send_sem=send_sem.at[g, number, by - 1],
                recv_sem=recv_sem.at[g, number, by - 1],
                device_id=device_of(moved(at, order[number], by), core),
                device_id_type=MESH,
            )
            copy.start()
            copies.append(copy)
        return copies

    def sibling(g):
        part = view(buf, g, at, core, (0, 1, 2))
        copy = pltpu.make_async_remote_copy(
            src_ref=part,
            dst_ref=part,
            send_sem=sib_sems.at[0, g],
            recv_sem=sib_sems.at[1, g],
            device_id=device_of(at, 1 - core),
            device_id_type=MESH,
        )
        copy.start()
        return copy

    flights = {}
    for step in range(GROUPS + 3):
        if step < GROUPS:
            own[step].wait()
            flights[step, 0] = phase(step, 0)
        for number in (1, 2, 3):
            g = step - number
            if 0 <= g < GROUPS:
                for copy in flights[g, number - 1]:
                    copy.wait_recv()
                if number < 3:
                    flights[g, number] = phase(g, number)
                else:
                    flights[g, 3] = [sibling(g)]
    for g in range(GROUPS):
        for number in range(3):
            for copy in flights[g, number]:
                copy.wait_send()
        flights[g, 3][0].wait()


def gather(weight):
    rows, columns = weight.shape
    out = pl.pallas_call(
        gather_kernel,
        out_shape=jax.ShapeDtypeStruct((GROUPS, 2, 4, 4, 2, 2, rows, GCOLS), weight.dtype),
        in_specs=[pl.BlockSpec(memory_space=pl.ANY)],
        out_specs=pl.BlockSpec(memory_space=pl.ANY),
        scratch_shapes=[
            pltpu.SemaphoreType.DMA((GROUPS,)),
            pltpu.SemaphoreType.DMA((GROUPS, 3, 3)),
            pltpu.SemaphoreType.DMA((GROUPS, 3, 3)),
            pltpu.SemaphoreType.DMA((2, GROUPS)),
        ],
        compiler_params=pltpu.CompilerParams(collective_id=0, has_side_effects=True),
    )(weight)
    return out.reshape(GROUPS, rows * 128, GCOLS)


def scan_kernel(reverse, part_ref, out_ref, inbox, outbox, send_sem, recv_sem):
    me = lax.axis_index("ctx")
    dp = lax.axis_index("dp")
    barrier = pltpu.get_barrier_semaphore()

    def greet(step, carry):
        pl.semaphore_signal(
            barrier, 1, device_id=(lax.rem(me + step, N_CTX), dp), device_id_type=MESH
        )
        return carry

    lax.fori_loop(1, N_CTX, greet, 0)
    pl.semaphore_wait(barrier, N_CTX - 1)

    def exchange(src, dst, number):
        def send(step, carry):
            other = lax.rem(me + step, N_CTX)
            pltpu.make_async_remote_copy(
                src_ref=src.at[other],
                dst_ref=dst.at[me],
                send_sem=send_sem.at[number],
                recv_sem=recv_sem.at[number],
                device_id=(other, dp),
                device_id_type=MESH,
            ).start()
            return carry

        lax.fori_loop(1, N_CTX, send, 0)
        dst[pl.ds(me, 1)] = src[pl.ds(me, 1)]
        most = pl.ds(0, N_CTX - 1)
        pltpu.make_async_copy(src.at[most], dst.at[most], recv_sem.at[number]).wait()
        pltpu.make_async_copy(src.at[most], dst.at[most], send_sem.at[number]).wait()

    exchange(part_ref, inbox, 0)

    def add(step, total):
        source = N_CTX - 1 - step if reverse else step
        outbox[source] = total.astype(outbox.dtype)
        return total + inbox[source].astype(jnp.float32)

    lax.fori_loop(0, N_CTX, add, jnp.zeros(inbox.shape[1:], jnp.float32))
    exchange(outbox, out_ref, 1)


def entering(part, reverse, number):
    pieces = part.astype(jnp.bfloat16).reshape(N_CTX, PIECE, HEAD)
    out = pl.pallas_call(
        functools.partial(scan_kernel, reverse),
        out_shape=jax.ShapeDtypeStruct(pieces.shape, pieces.dtype),
        in_specs=[pl.BlockSpec(memory_space=pltpu.VMEM)],
        out_specs=pl.BlockSpec(memory_space=pltpu.VMEM),
        scratch_shapes=[
            pltpu.VMEM(pieces.shape, pieces.dtype),
            pltpu.VMEM(pieces.shape, pieces.dtype),
            pltpu.SemaphoreType.DMA((2,)),
            pltpu.SemaphoreType.DMA((2,)),
        ],
        compiler_params=pltpu.CompilerParams(collective_id=number, has_side_effects=True),
    )(pieces)
    return out.reshape(part.shape)


def per_device(tokens, key_input, values, q_weight, q_spikes, k_spikes, cotangent):
    batches, length, model_width = tokens.shape
    head_total = q_weight.shape[1]
    sequence = length * lax.axis_size("ctx")
    factor = 3.0 / math.sqrt(HEAD * sequence)
    wide_float = jnp.float32
    token_rows = tokens.reshape(batches * length, model_width)
    spiked_keys = key_input * k_spikes.astype(jnp.bfloat16)

    def by_heads(array):
        return array.reshape(batches, length, HEADS, HEAD)

    key_wide = by_heads(spiked_keys)
    value_wide = by_heads(values)
    grad_wide = by_heads(cotangent)
    own_memory = jnp.einsum(
        "blhe,blhf->bhef", key_wide, value_wide, preferred_element_type=wide_float
    )
    before = entering(own_memory, False, 1)
    weight = gather(q_weight)
    projected = jnp.einsum("td,gdf->tgf", token_rows, weight, preferred_element_type=jnp.float32)
    queries = (
        projected.reshape(batches, length, head_total) * q_spikes.astype(jnp.float32)
    ).astype(jnp.bfloat16)
    query_wide = by_heads(queries)
    own_adjoint = jnp.einsum(
        "blhe,blhf->bhef", query_wide, grad_wide, preferred_element_type=wide_float
    )
    later_adjoint = entering(own_adjoint, True, 2)
    causal = jnp.tril(jnp.ones((length, length), jnp.float32))
    scores = jnp.einsum("blhe,bmhe->bhlm", query_wide, key_wide, preferred_element_type=wide_float)
    scores = (scores * causal).astype(jnp.bfloat16)
    grad_scores = jnp.einsum(
        "blhf,bmhf->bhlm", grad_wide, value_wide, preferred_element_type=wide_float
    )
    grad_scores = (grad_scores * causal).astype(jnp.bfloat16)
    output = jnp.einsum("bhlm,bmhf->blhf", scores, value_wide, preferred_element_type=wide_float)
    output = output + jnp.einsum(
        "blhe,bhef->blhf", query_wide, before, preferred_element_type=wide_float
    )
    query_grad = jnp.einsum(
        "bhlm,bmhe->blhe", grad_scores, key_wide, preferred_element_type=wide_float
    )
    query_grad = query_grad + jnp.einsum(
        "blhf,bhef->blhe", grad_wide, before, preferred_element_type=wide_float
    )
    key_grad = jnp.einsum(
        "bhlm,blhe->bmhe", grad_scores, query_wide, preferred_element_type=wide_float
    )
    key_grad = key_grad + jnp.einsum(
        "bmhf,bhef->bmhe", value_wide, later_adjoint, preferred_element_type=wide_float
    )
    value_grad = jnp.einsum("bhlm,blhf->bmhf", scores, grad_wide, preferred_element_type=wide_float)
    value_grad = value_grad + jnp.einsum(
        "bmhe,bhef->bmhf", key_wide, later_adjoint, preferred_element_type=wide_float
    )
    shape_out = (batches, length, head_total)
    attended = (factor * output.reshape(shape_out)).astype(jnp.bfloat16)
    masked_grad = (factor * query_grad.reshape(shape_out) * q_spikes.astype(jnp.float32)).astype(
        jnp.bfloat16
    )
    masked_rows = masked_grad.reshape(batches * length, GROUPS, GCOLS)
    token_grad = jnp.einsum("tgf,gdf->td", masked_rows, weight, preferred_element_type=jnp.float32)
    grad_tokens = token_grad.reshape(batches, length, model_width).astype(jnp.bfloat16)
    grad_keys = (factor * key_grad.reshape(shape_out) * k_spikes.astype(jnp.float32)).astype(
        jnp.bfloat16
    )
    grad_values = (factor * value_grad.reshape(shape_out)).astype(jnp.bfloat16)
    return (attended, grad_tokens, grad_keys, grad_values)


def solution(mesh):
    rows = P("dp", "ctx", None)
    in_specs = (rows, rows, rows, P(("ctx", "dp"), None), rows, rows, rows)
    return jax.shard_map(
        per_device, mesh=mesh, in_specs=in_specs, out_specs=(rows,) * 4, check_vma=False
    )
```

```python
import functools
import math

import jax
import jax.numpy as jnp
from jax import lax
from jax.experimental import pallas as pl
from jax.experimental.pallas import tpu as pltpu
from jax.sharding import PartitionSpec as P

HEADS = 16
HEAD = 128
TOK = 384
D = 4096
HD = HEADS * HEAD
GROUPS = 8
GCOLS = 256
N_CTX = 32
ROWS = 32
FIRST = 12
MESH = pl.DeviceIdType.MESH
ORDERS = ((0, 1, 2), (1, 2, 0), (2, 0, 1))
BF16 = jnp.bfloat16
F32 = jnp.float32
NT = (((1,), (1,)), ((), ()))
TN = (((0,), (0,)), ((), ()))


def place():
    ctx = lax.axis_index("ctx")
    dp = lax.axis_index("dp")
    x = lax.rem(ctx, 4)
    y = lax.rem(ctx // 4, 4)
    z = (dp // 2) * 2 + ctx // 16
    return (x, y, z), lax.rem(dp, 2)


def device_of(at, core):
    x, y, z = at
    return (lax.rem(z, 2) * 16 + y * 4 + x, (z // 2) * 2 + core)


def moved(at, axis, by):
    out = list(at)
    out[axis] = lax.rem(out[axis] + by, 4)
    return tuple(out)


def view(buf, group, at, core, whole, half=None):
    picks = []
    for axis in range(2):
        if half is not None and half[0] == axis:
            picks.append(pl.ds(2 * half[1], 2))
        elif axis in whole:
            picks.append(slice(None))
        else:
            picks.append(at[axis])
    low = slice(None) if 2 in whole else lax.rem(at[2], 2)
    high = slice(None) if 2 in whole else at[2] // 2
    return buf.at[group, low, picks[1], picks[0], high, core]


def dot(a, b, dims=(((1,), (0,)), ((), ()))):
    return lax.dot_general(a, b, dims, preferred_element_type=F32)


def layer_kernel(
    factor,
    tok_hbm,
    key_hbm,
    val_hbm,
    w_hbm,
    qsp_hbm,
    ksp_hbm,
    cot_hbm,
    att_hbm,
    gtok_hbm,
    gkey_hbm,
    gval_hbm,
    wbuf,
    tok,
    keys,
    val,
    cot,
    qsp,
    ksp,
    mg,
    kgrad,
    vgrad,
    att,
    gtok,
    gkey,
    gval,
    m_send,
    m_in,
    m_out,
    m_state,
    a_send,
    a_in,
    a_out,
    a_state,
    b_send,
    b_in,
    b_out,
    b_state,
    own_sem,
    load_sem,
    send_sem,
    recv_sem,
    sib_sem,
    scan_sem,
    store_sem,
):
    at, core = place()
    ctx = lax.axis_index("ctx")
    dp = lax.axis_index("dp")
    other_core = device_of(at, 1 - core)

    own = []
    for g in range(GROUPS):
        copy = pltpu.make_async_copy(
            w_hbm.at[:, pl.ds(g * GCOLS, GCOLS)], view(wbuf, g, at, core, ()), own_sem.at[g]
        )
        copy.start()
        own.append(copy)

    loads = []
    for number, (src, dst) in enumerate(
        (
            (key_hbm, keys),
            (ksp_hbm, ksp),
            (val_hbm, val),
            (cot_hbm, cot),
            (tok_hbm, tok),
            (qsp_hbm, qsp),
        )
    ):
        copy = pltpu.make_async_copy(src, dst, load_sem.at[number])
        copy.start()
        loads.append(copy)

    barrier = pltpu.get_barrier_semaphore()

    def greet(step, carry):
        pl.semaphore_signal(
            barrier, 1, device_id=(lax.rem(ctx + step, N_CTX), dp), device_id_type=MESH
        )
        return carry

    lax.fori_loop(1, N_CTX, greet, 0)
    far_z = 1 - at[2] // 2
    for low in (0, 1):
        pl.semaphore_signal(
            barrier,
            1,
            device_id=(low * 16 + at[1] * 4 + at[0], far_z * 2 + core),
            device_id_type=MESH,
        )
    pl.semaphore_signal(barrier, 1, device_id=other_core, device_id_type=MESH)
    pl.semaphore_wait(barrier, N_CTX + 2)

    ended = []

    def send(part, g, slot, target):
        copy = pltpu.make_async_remote_copy(
            src_ref=part,
            dst_ref=part,
            send_sem=send_sem.at[g, slot],
            recv_sem=recv_sem.at[g, slot],
            device_id=target,
            device_id_type=MESH,
        )
        copy.start()
        ended.append(copy)
        return copy

    def spread(g, number):
        order = ORDERS[g % 3]
        part = view(wbuf, g, at, core, order[:number])
        return [
            send(part, g, 3 * number + by - 1, device_of(moved(at, order[number], by), core))
            for by in (1, 3, 2)
        ]

    def to_sibling(g, slot, where):
        part = view(wbuf, g, where, core, ORDERS[g % 3][:2])
        copy = pltpu.make_async_remote_copy(
            src_ref=part,
            dst_ref=part,
            send_sem=sib_sem.at[0, g, slot],
            recv_sem=sib_sem.at[1, g, slot],
            device_id=other_core,
            device_id_type=MESH,
        )
        copy.start()
        ended.append(copy)
        return copy

    flights = {}

    def first(g):
        own[g].wait()
        flights[g, 0] = spread(g, 0)

    def second(g):
        for copy in flights[g, 0]:
            copy.wait_recv()
        flights[g, 1] = spread(g, 1)

    def third(g):
        for copy in flights[g, 1]:
            copy.wait_recv()
        order = ORDERS[g % 3]
        part = view(wbuf, g, at, core, order[:2])
        flights[g, 2] = [
            send(part, g, 6, device_of(moved(at, order[2], 1), core)),
            send(part, g, 7, device_of(moved(at, order[2], 3), core)),
        ]
        flights[g, 4] = [to_sibling(g, 0, at)]

    def fourth(g):
        order = ORDERS[g % 3]
        left, right = moved(at, order[2], 3), moved(at, order[2], 1)
        split = 0 if order[2] == 1 else 1
        flights[g, 2][0].wait_recv()
        one = send(
            view(wbuf, g, left, core, order[:2], (split, 0)), g, 8, device_of(right, core)
        )
        flights[g, 4].append(to_sibling(g, 1, left))
        flights[g, 2][1].wait_recv()
        two = send(
            view(wbuf, g, right, core, order[:2], (split, 1)), g, 9, device_of(left, core)
        )
        flights[g, 4].append(to_sibling(g, 2, right))
        flights[g, 3] = [one, two]

    def fifth(g):
        for copy in flights[g, 3]:
            copy.wait_recv()
        flights[g, 4].append(to_sibling(g, 3, moved(at, ORDERS[g % 3][2], 2)))

    def arrived(g):
        for copy in flights[g, 4]:
            copy.wait_recv()

    def exchange(src, dst, number, tiles):
        def one(step, carry):
            other = lax.rem(ctx + step, N_CTX)
            pltpu.make_async_remote_copy(
                src_ref=src.at[pl.ds(other * tiles, tiles)],
                dst_ref=dst.at[pl.ds(ctx * tiles, tiles)],
                send_sem=scan_sem.at[0, number],
                recv_sem=scan_sem.at[1, number],
                device_id=(other, dp),
                device_id_type=MESH,
            ).start()
            return carry

        lax.fori_loop(1, N_CTX, one, 0)
        dst[pl.ds(ctx * tiles, tiles)] = src[pl.ds(ctx * tiles, tiles)]

    def exchanged(src, dst, number, tiles):
        most = pl.ds(0, (N_CTX - 1) * tiles)
        pltpu.make_async_copy(src.at[most], dst.at[most], scan_sem.at[1, number]).wait()
        pltpu.make_async_copy(src.at[most], dst.at[most], scan_sem.at[0, number]).wait()

    def prefix(inbox, outbox, tiles, reverse):
        def add(step, total):
            source = N_CTX - 1 - step if reverse else step
            outbox[pl.ds(source * tiles, tiles)] = total.astype(BF16)
            return total + inbox[pl.ds(source * tiles, tiles)].astype(F32)

        lax.fori_loop(0, N_CTX, add, jnp.zeros((tiles, 16, HEAD), F32))

    def columns(head):
        return pl.ds(pl.multiple_of(head * HEAD, HEAD), HEAD)

    def lower():
        rows = lax.broadcasted_iota(jnp.int32, (TOK, TOK), 0)
        return rows >= lax.broadcasted_iota(jnp.int32, (TOK, TOK), 1)

    def upper():
        rows = lax.broadcasted_iota(jnp.int32, (TOK, TOK), 0)
        return rows <= lax.broadcasted_iota(jnp.int32, (TOK, TOK), 1)

    def own_memory(head, carry):
        cols = columns(head)
        k = (keys[:, cols].astype(F32) * ksp[:, cols].astype(F32)).astype(BF16)
        keys[:, cols] = k
        state = dot(k, val[:, cols], TN).astype(BF16)
        m_send[pl.ds(head * 8, 8)] = state.reshape(8, 16, HEAD)
        return carry

    def own_query_grad(head, carry):
        cols = columns(head)
        grad_scores = jnp.where(lower(), dot(cot[:, cols], val[:, cols], NT), 0.0).astype(BF16)
        vgrad[:, cols] = dot(grad_scores, keys[:, cols])
        return carry

    def mask_grad(head, carry):
        cols = columns(head)
        state = m_state[pl.ds(head * 8, 8)].reshape(HEAD, HEAD)
        whole = vgrad[:, cols] + dot(cot[:, cols], state, NT)
        mg[:, cols] = (factor * whole * qsp[:, cols].astype(F32)).astype(BF16)
        return carry

    def attend(g):
        weight = wbuf[g].reshape(D, GCOLS)
        both = dot(tok[...], weight)
        for one in range(2):
            head = 2 * g + one
            cols = columns(head)
            q = both[:, one * HEAD : (one + 1) * HEAD] * qsp[:, cols].astype(F32)
            q = q.astype(BF16)
            k, v, c = keys[:, cols], val[:, cols], cot[:, cols]
            state = dot(q, c, TN).astype(BF16).reshape(8, 16, HEAD)
            if head < FIRST:
                a_send[pl.ds(head * 8, 8)] = state
            else:
                b_send[pl.ds((head - FIRST) * 8, 8)] = state
            scores = jnp.where(lower(), dot(q, k, NT), 0.0).astype(BF16)
            memory = m_state[pl.ds(head * 8, 8)].reshape(HEAD, HEAD)
            att[:, cols] = (factor * (dot(scores, v) + dot(q, memory))).astype(BF16)
            scores = jnp.where(upper(), dot(k, q, NT), 0.0).astype(BF16)
            vgrad[:, cols] = dot(scores, c)
            grad_scores = jnp.where(upper(), dot(v, c, NT), 0.0).astype(BF16)
            kgrad[:, cols] = dot(grad_scores, q)

    stores = []

    def token_grad(number, carry):
        low, y, pair = number // 8, lax.rem(number // 2, 4), lax.rem(number, 2)
        total = None
        for g in range(GROUPS):
            weight = wbuf[g, low, y, pl.ds(2 * pair, 2)].reshape(GCOLS, GCOLS)
            term = dot(mg[:, g * GCOLS : (g + 1) * GCOLS], weight, NT)
            total = term if total is None else total + term
        cols = pl.ds(pl.multiple_of(number * GCOLS, GCOLS), GCOLS)
        gtok[:, cols] = total.astype(BF16)
        return carry

    def finish(states, first_head):
        def one(head, carry):
            cols = columns(head)
            state = states[pl.ds((head - first_head) * 8, 8)].reshape(HEAD, HEAD)
            key_grad = kgrad[:, cols] + dot(val[:, cols], state, NT)
            gkey[:, cols] = (factor * key_grad * ksp[:, cols].astype(F32)).astype(BF16)
            value_grad = vgrad[:, cols] + dot(keys[:, cols], state)
            gval[:, cols] = (factor * value_grad).astype(BF16)
            return carry

        return one

    def store(src, dst, number):
        copy = pltpu.make_async_copy(src, dst, store_sem.at[number])
        copy.start()
        stores.append(copy)

    m_tiles, a_tiles, b_tiles = HEADS // 4, FIRST // 4, (HEADS - FIRST) // 4
    for g in range(GROUPS):
        first(g)
    for number in range(3):
        loads[number].wait()
    lax.fori_loop(0, HEADS, own_memory, 0)
    exchange(m_send, m_in, 0, m_tiles)
    for step in range(GROUPS + 7):
        if step < GROUPS:
            second(step)
        if 0 <= step - 1 < GROUPS:
            third(step - 1)
        if 0 <= step - 4 < GROUPS:
            fourth(step - 4)
        if 0 <= step - 6 < GROUPS:
            fifth(step - 6)
        if step == 0:
            loads[3].wait()
        if step < 4:
            lax.fori_loop(4 * step, 4 * step + 4, own_query_grad, 0)
        if step == 3:
            exchanged(m_send, m_in, 0, m_tiles)
            prefix(m_in, m_out, m_tiles, False)
            exchange(m_out, m_state, 1, m_tiles)
        if step == 6:
            exchanged(m_out, m_state, 1, m_tiles)
            loads[4].wait()
            loads[5].wait()
            lax.fori_loop(0, HEADS, mask_grad, 0)
        if 0 <= step - 7 < GROUPS:
            arrived(step - 7)
            attend(step - 7)
        if 2 * (step - 6) == FIRST:
            exchange(a_send, a_in, 2, a_tiles)
        if 2 * (step - 7) == FIRST:
            exchanged(a_send, a_in, 2, a_tiles)
            prefix(a_in, a_out, a_tiles, True)
            exchange(a_out, a_state, 3, a_tiles)
    exchange(b_send, b_in, 4, b_tiles)
    store(att, att_hbm, 0)
    lax.fori_loop(0, 5, token_grad, 0)
    exchanged(b_send, b_in, 4, b_tiles)
    prefix(b_in, b_out, b_tiles, True)
    exchange(b_out, b_state, 5, b_tiles)
    lax.fori_loop(5, 16, token_grad, 0)
    store(gtok, gtok_hbm, 1)
    exchanged(a_out, a_state, 3, a_tiles)
    lax.fori_loop(0, FIRST, finish(a_state, 0), 0)
    exchanged(b_out, b_state, 5, b_tiles)
    lax.fori_loop(FIRST, HEADS, finish(b_state, FIRST), 0)
    store(gkey, gkey_hbm, 2)
    store(gval, gval_hbm, 3)
    for copy in ended:
        copy.wait_send()
    for copy in stores:
        copy.wait()


def scan_buffers(heads):
    return [pltpu.VMEM((heads * 8, 16, HEAD), BF16)] * 4


def layer(factor, tokens, key_input, values, q_weight, q_spikes, k_spikes, cotangent):
    wide = pltpu.VMEM((TOK, HD), BF16)
    wide_float = pltpu.VMEM((TOK, HD), F32)
    wide_int = pltpu.VMEM((TOK, HD), jnp.int32)
    anywhere = pl.BlockSpec(memory_space=pl.ANY)
    narrow = jax.ShapeDtypeStruct((TOK, HD), BF16)
    return pl.pallas_call(
        functools.partial(layer_kernel, factor),
        out_shape=(narrow, jax.ShapeDtypeStruct((TOK, D), BF16), narrow, narrow),
        in_specs=[anywhere] * 7,
        out_specs=(anywhere,) * 4,
        scratch_shapes=[
            pltpu.VMEM((GROUPS, 2, 4, 4, 2, 2, ROWS, GCOLS), BF16),
            pltpu.VMEM((TOK, D), BF16),
            wide,
            wide,
            wide,
            wide_int,
            wide_int,
            wide,
            wide_float,
            wide_float,
            wide,
            pltpu.VMEM((TOK, D), BF16),
            wide,
            wide,
            *scan_buffers(HEADS),
            *scan_buffers(FIRST),
            *scan_buffers(HEADS - FIRST),
            pltpu.SemaphoreType.DMA((GROUPS,)),
            pltpu.SemaphoreType.DMA((6,)),
            pltpu.SemaphoreType.DMA((GROUPS, 10)),
            pltpu.SemaphoreType.DMA((GROUPS, 10)),
            pltpu.SemaphoreType.DMA((2, GROUPS, 4)),
            pltpu.SemaphoreType.DMA((2, 6)),
            pltpu.SemaphoreType.DMA((4,)),
        ],
        compiler_params=pltpu.CompilerParams(
            collective_id=0, has_side_effects=True, vmem_limit_bytes=60 << 20
        ),
    )(tokens, key_input, values, q_weight, q_spikes, k_spikes, cotangent)


def per_device(tokens, key_input, values, q_weight, q_spikes, k_spikes, cotangent):
    sequence = tokens.shape[1] * lax.axis_size("ctx")
    factor = 3.0 / math.sqrt(HEAD * sequence)
    outs = layer(
        factor, tokens[0], key_input[0], values[0], q_weight, q_spikes[0], k_spikes[0], cotangent[0]
    )
    return tuple(out[None] for out in outs)


def solution(mesh):
    rows = P("dp", "ctx", None)
    in_specs = (rows, rows, rows, P(("ctx", "dp"), None), rows, rows, rows)
    return jax.shard_map(
        per_device, mesh=mesh, in_specs=in_specs, out_specs=(rows,) * 4, check_vma=False
    )
```

```python
import functools
import math

import jax
import jax.numpy as jnp
from jax import lax
from jax.experimental import pallas as pl
from jax.experimental.pallas import tpu as pltpu
from jax.sharding import PartitionSpec as P

HEADS = 16
HEAD = 128
TOK = 384
D = 4096
HD = HEADS * HEAD
GROUPS = 8
GCOLS = 256
N_CTX = 32
ROWS = 32
FIRST = 12
CHUNK = 512
AHEAD = 3
LAGS = (0, 3, 5, 6)
MESH = pl.DeviceIdType.MESH
ORDERS = ((0, 1, 2), (1, 2, 0), (2, 0, 1))
BF16 = jnp.bfloat16
F32 = jnp.float32
NT = (((1,), (1,)), ((), ()))
TN = (((0,), (0,)), ((), ()))


def place():
    ctx = lax.axis_index("ctx")
    dp = lax.axis_index("dp")
    x = lax.rem(ctx, 4)
    y = lax.rem(ctx // 4, 4)
    z = (dp // 2) * 2 + ctx // 16
    return (x, y, z), lax.rem(dp, 2)


def device_of(at, core):
    x, y, z = at
    return (lax.rem(z, 2) * 16 + y * 4 + x, (z // 2) * 2 + core)


def moved(at, axis, by):
    out = list(at)
    out[axis] = lax.rem(out[axis] + by, 4)
    return tuple(out)


def view(buf, group, at, core, whole, half=None):
    picks = []
    for axis in range(2):
        if half is not None and half[0] == axis:
            picks.append(pl.ds(2 * half[1], 2))
        elif axis in whole:
            picks.append(slice(None))
        else:
            picks.append(at[axis])
    low = slice(None) if 2 in whole else lax.rem(at[2], 2)
    high = slice(None) if 2 in whole else at[2] // 2
    return buf.at[group, low, picks[1], picks[0], high, core]


def dot(a, b, dims=(((1,), (0,)), ((), ()))):
    return lax.dot_general(a, b, dims, preferred_element_type=F32)


def layer_kernel(
    factor,
    tok_hbm,
    key_hbm,
    val_hbm,
    w_hbm,
    qsp_hbm,
    ksp_hbm,
    cot_hbm,
    att,
    gtok,
    gkey,
    gval,
    wbuf,
    tok,
    keys,
    val,
    cot,
    qsp,
    ksp,
    mg,
    kgrad,
    vgrad,
    qgrad,
    projected,
    queries,
    local,
    m_send,
    m_in,
    m_out,
    m_state,
    a_send,
    a_in,
    a_out,
    a_state,
    own_sem,
    load_sem,
    send_sem,
    recv_sem,
    sib_sem,
    scan_sem,
):
    at, core = place()
    ctx = lax.axis_index("ctx")
    dp = lax.axis_index("dp")
    other_core = device_of(at, 1 - core)

    own = []
    for g in range(GROUPS):
        copy = pltpu.make_async_copy(
            w_hbm.at[:, pl.ds(g * GCOLS, GCOLS)], view(wbuf, g, at, core, ()), own_sem.at[g]
        )
        copy.start()
        own.append(copy)

    loads = []
    for number, (src, dst) in enumerate(
        (
            (key_hbm, keys),
            (ksp_hbm, ksp),
            (val_hbm, val),
            (cot_hbm, cot),
            (tok_hbm, tok),
            (qsp_hbm, qsp),
        )
    ):
        copy = pltpu.make_async_copy(src, dst, load_sem.at[number])
        copy.start()
        loads.append(copy)

    barrier = pltpu.get_barrier_semaphore()

    def greet(step, carry):
        pl.semaphore_signal(
            barrier, 1, device_id=(lax.rem(ctx + step, N_CTX), dp), device_id_type=MESH
        )
        return carry

    lax.fori_loop(1, N_CTX, greet, 0)
    far_z = 1 - at[2] // 2
    for low in (0, 1):
        pl.semaphore_signal(
            barrier,
            1,
            device_id=(low * 16 + at[1] * 4 + at[0], far_z * 2 + core),
            device_id_type=MESH,
        )
    pl.semaphore_signal(barrier, 1, device_id=other_core, device_id_type=MESH)
    pl.semaphore_wait(barrier, N_CTX + 2)

    def remote(part, sems, target):
        return pltpu.make_async_remote_copy(
            src_ref=part,
            dst_ref=part,
            send_sem=sems[0],
            recv_sem=sems[1],
            device_id=target,
            device_id_type=MESH,
        )

    def link(part, g, slot, target):
        return remote(part, (send_sem.at[g, slot], recv_sem.at[g, slot]), target)

    def spread(g, order, number):
        part = view(wbuf, g, at, core, order[:number])
        return [
            link(part, g, 3 * number + by - 1, device_of(moved(at, order[number], by), core))
            for by in (1, 3, 2)
        ]

    def near(g, order):
        part = view(wbuf, g, at, core, order[:2])
        return [
            link(part, g, 5 + way, device_of(moved(at, order[2], by), core))
            for way, by in ((1, 1), (2, 3))
        ]

    def far(g, order):
        left, right = moved(at, order[2], 3), moved(at, order[2], 1)
        split = 0 if order[2] == 1 else 1
        return [
            link(view(wbuf, g, here, core, order[:2], (split, half)), g, 8 + half, device_of(to, core))
            for half, here, to in ((0, left, right), (1, right, left))
        ]

    def sibling(g, order):
        return [
            remote(
                view(wbuf, g, moved(at, order[2], by), core, order[:2]),
                (sib_sem.at[0, g, by], sib_sem.at[1, g, by]),
                other_core,
            )
            for by in range(4)
        ]

    def ordered(g, act):
        for number, order in enumerate(ORDERS):

            @pl.when(lax.rem(g + core, 3) == number)
            def _(order=order):
                act(g, order)

    def start(copies):
        for copy in copies:
            copy.start()

    def first(g, order):
        start(spread(g, order, 0))

    def second(g, order):
        for copy in spread(g, order, 0):
            copy.wait_recv()
        start(spread(g, order, 1))

    def third(g, order):
        for copy in spread(g, order, 1):
            copy.wait_recv()
        start(near(g, order))
        sibling(g, order)[0].start()

    def fourth(g, order):
        arriving, onward, across = near(g, order), far(g, order), sibling(g, order)
        for half, by in ((0, 3), (1, 1)):
            arriving[half].wait_recv()
            onward[half].start()
            across[by].start()

    def fifth(g, order):
        for copy in far(g, order):
            copy.wait_recv()
        sibling(g, order)[2].start()

    def arrived(g, order):
        for copy in sibling(g, order):
            copy.wait_recv()

    def sent(g, order):
        for copy in (
            *spread(g, order, 0),
            *spread(g, order, 1),
            *near(g, order),
            *far(g, order),
            *sibling(g, order),
        ):
            copy.wait_send()

    def exchange(src, dst, number, tiles, base=0):
        def one(step, carry):
            other = lax.rem(ctx + step, N_CTX)
            pltpu.make_async_remote_copy(
                src_ref=src.at[pl.ds(base + other * tiles, tiles)],
                dst_ref=dst.at[pl.ds(base + ctx * tiles, tiles)],
                send_sem=scan_sem.at[0, number],
                recv_sem=scan_sem.at[1, number],
                device_id=(other, dp),
                device_id_type=MESH,
            ).start()
            return carry

        lax.fori_loop(1, N_CTX, one, 0)
        mine = pl.ds(base + ctx * tiles, tiles)
        dst[mine] = src[mine]

    def exchanged(src, dst, number, tiles, base=0):
        most = pl.ds(base, (N_CTX - 1) * tiles)
        pltpu.make_async_copy(src.at[most], dst.at[most], scan_sem.at[1, number]).wait()
        pltpu.make_async_copy(src.at[most], dst.at[most], scan_sem.at[0, number]).wait()

    def prefix(inbox, outbox, tiles, reverse, base=0):
        def add(step, total):
            source = N_CTX - 1 - step if reverse else step
            piece = pl.ds(base + source * tiles, tiles)
            outbox[piece] = total.astype(BF16)
            return total + inbox[piece].astype(F32)

        lax.fori_loop(0, N_CTX, add, jnp.zeros((tiles, 16, HEAD), F32))

    def columns(head):
        return pl.ds(pl.multiple_of(head * HEAD, HEAD), HEAD)

    def keep(product, first_row, first_col, below):
        rows = lax.broadcasted_iota(jnp.int32, product.shape, 0) + first_row
        cols = lax.broadcasted_iota(jnp.int32, product.shape, 1) + first_col
        return jnp.where(rows >= cols if below else rows <= cols, product, 0.0).astype(BF16)

    def below(a, b, c):
        wide = dot(keep(dot(a, b[:256], NT), 0, 0, True), c[:256])
        last = dot(keep(dot(a[256:], b[256:], NT), 0, 0, True), c[256:])
        return jnp.concatenate([wide[:256], wide[256:] + last], axis=0)

    def above(a, b, c):
        wide = dot(keep(dot(a, b[128:], NT), 0, 128, False), c[128:])
        head = dot(keep(dot(a[:128], b[:128], NT), 0, 0, False), c[:128])
        return jnp.concatenate([wide[:128] + head, wide[128:]], axis=0)

    def own_memory(head, carry):
        cols = columns(head)
        k = (keys[:, cols].astype(F32) * ksp[:, cols].astype(F32)).astype(BF16)
        keys[:, cols] = k
        state = dot(k, val[:, cols], TN).astype(BF16)
        m_send[pl.ds(head * 8, 8)] = state.reshape(8, 16, HEAD)
        return carry

    def own_query_grad(head, carry):
        cols = columns(head)
        qgrad[:, cols] = below(cot[:, cols], val[:, cols], keys[:, cols])
        return carry

    def use_memory(head, carry):
        cols = columns(head)
        state = m_state[pl.ds(head * 8, 8)].reshape(HEAD, HEAD)
        whole = qgrad[:, cols] + dot(cot[:, cols], state, NT)
        mg[:, cols] = (factor * whole * qsp[:, cols].astype(F32)).astype(BF16)
        att[:, cols] = (factor * (local[:, cols] + dot(queries[:, cols], state))).astype(BF16)
        return carry

    def project(g):
        projected[...] = dot(tok[...], wbuf[g].reshape(D, GCOLS))

    def attend(g):
        for one in range(2):
            head = 2 * g + one
            cols = columns(head)
            q = projected[:, one * HEAD : (one + 1) * HEAD] * qsp[:, cols].astype(F32)
            q = q.astype(BF16)
            queries[:, cols] = q
            k, v, c = keys[:, cols], val[:, cols], cot[:, cols]
            state = dot(q, c, TN).astype(BF16).reshape(8, 16, HEAD)
            a_send[pl.ds(head * 8, 8)] = state
            local[:, cols] = below(q, k, v)
            vgrad[:, cols] = above(k, q, c)
            kgrad[:, cols] = above(v, c, q)

    def token_grad(number, carry):
        pieces = [
            wbuf[g, number // 4, lax.rem(number, 4)].reshape(CHUNK, GCOLS) for g in range(GROUPS)
        ]
        total = dot(mg[...], jnp.concatenate(pieces, axis=1), NT)
        cols = pl.ds(pl.multiple_of(number * CHUNK, CHUNK), CHUNK)
        gtok[:, cols] = total.astype(BF16)
        return carry

    def finish(head, carry):
        cols = columns(head)
        state = a_state[pl.ds(head * 8, 8)].reshape(HEAD, HEAD)
        key_grad = kgrad[:, cols] + dot(val[:, cols], state, NT)
        gkey[:, cols] = (factor * key_grad * ksp[:, cols].astype(F32)).astype(BF16)
        value_grad = vgrad[:, cols] + dot(keys[:, cols], state)
        gval[:, cols] = (factor * value_grad).astype(BF16)
        return carry

    m_tiles, a_tiles, b_tiles = HEADS // 4, FIRST // 4, (HEADS - FIRST) // 4
    b_base = FIRST * 8
    for copy in own:
        copy.wait()

    def begin(g, carry):
        ordered(g, first)
        return carry

    lax.fori_loop(0, GROUPS, begin, 0)
    for number in range(4):
        loads[number].wait()
    lax.fori_loop(0, HEADS, own_memory, 0, unroll=2)

    def ahead(g, carry):
        ordered(g, second)
        return carry

    lax.fori_loop(0, AHEAD, ahead, 0)
    exchange(m_send, m_in, 0, m_tiles)

    def body(step, carry):
        for lag, act in zip((-AHEAD, *LAGS), (second, third, fourth, fifth, arrived)):
            low = max(lag, 0)

            @pl.when((step >= low) & (step < lag + GROUPS))
            def _(lag=lag, act=act):
                ordered(step - lag, act)

        last = LAGS[3]

        @pl.when(step < 4)
        def _():
            for pair in range(2):
                for one in range(2):
                    own_query_grad(4 * step + 2 * pair + one, 0)

        @pl.when(step == 5)
        def _():
            exchanged(m_send, m_in, 0, m_tiles)
            prefix(m_in, m_out, m_tiles, False)
            exchange(m_out, m_state, 1, m_tiles)

        @pl.when(step == last)
        def _():
            loads[4].wait()
            loads[5].wait()

        @pl.when(step >= last)
        def _():
            project(step - last)

        @pl.when((step >= last) & (step >= 0))
        def _():
            attend(step - last)

        @pl.when(2 * (step - last + 1) == FIRST)
        def _():
            exchange(a_send, a_in, 2, a_tiles)

        return carry

    lax.fori_loop(0, GROUPS + LAGS[3], body, 0)
    exchange(a_send, a_in, 4, b_tiles, b_base)
    exchanged(a_send, a_in, 2, a_tiles)
    prefix(a_in, a_out, a_tiles, True)
    exchange(a_out, a_state, 3, a_tiles)
    exchanged(m_out, m_state, 1, m_tiles)
    lax.fori_loop(0, HEADS, use_memory, 0, unroll=2)
    exchanged(a_send, a_in, 4, b_tiles, b_base)
    prefix(a_in, a_out, b_tiles, True, b_base)
    exchange(a_out, a_state, 5, b_tiles, b_base)
    lax.fori_loop(0, 8, token_grad, 0)
    exchanged(a_out, a_state, 3, a_tiles)
    lax.fori_loop(0, FIRST, finish, 0, unroll=2)
    exchanged(a_out, a_state, 5, b_tiles, b_base)
    lax.fori_loop(FIRST, HEADS, finish, 0, unroll=2)

    def end(g, carry):
        ordered(g, sent)
        return carry

    lax.fori_loop(0, GROUPS, end, 0)


def scan_buffers(heads):
    return [pltpu.VMEM((heads * 8, 16, HEAD), BF16)] * 4


def layer(factor, tokens, key_input, values, q_weight, q_spikes, k_spikes, cotangent):
    wide = pltpu.VMEM((TOK, HD), BF16)
    wide_float = pltpu.VMEM((TOK, HD), F32)
    wide_int = pltpu.VMEM((TOK, HD), jnp.int32)
    anywhere = pl.BlockSpec(memory_space=pl.ANY)
    return pl.pallas_call(
        functools.partial(layer_kernel, factor),
        out_shape=(wide, pltpu.VMEM((TOK, D), BF16), wide, wide),
        in_specs=[anywhere] * 7,
        out_specs=(pl.BlockSpec(memory_space=pltpu.VMEM),) * 4,
        scratch_shapes=[
            pltpu.VMEM((GROUPS, 2, 4, 4, 2, 2, ROWS, GCOLS), BF16),
            pltpu.VMEM((TOK, D), BF16),
            wide,
            wide,
            wide,
            wide_int,
            wide_int,
            wide,
            wide_float,
            wide_float,
            wide_float,
            pltpu.VMEM((TOK, GCOLS), F32),
            wide,
            wide_float,
            *scan_buffers(HEADS),
            *scan_buffers(HEADS),
            pltpu.SemaphoreType.DMA((GROUPS,)),
            pltpu.SemaphoreType.DMA((6,)),
            pltpu.SemaphoreType.DMA((GROUPS, 10)),
            pltpu.SemaphoreType.DMA((GROUPS, 10)),
            pltpu.SemaphoreType.DMA((2, GROUPS, 4)),
            pltpu.SemaphoreType.DMA((2, 6)),
        ],
        compiler_params=pltpu.CompilerParams(
            collective_id=0, has_side_effects=True, vmem_limit_bytes=54 << 20
        ),
    )(tokens, key_input, values, q_weight, q_spikes, k_spikes, cotangent)


def per_device(tokens, key_input, values, q_weight, q_spikes, k_spikes, cotangent):
    sequence = tokens.shape[1] * lax.axis_size("ctx")
    factor = 3.0 / math.sqrt(HEAD * sequence)
    outs = layer(
        factor, tokens[0], key_input[0], values[0], q_weight, q_spikes[0], k_spikes[0], cotangent[0]
    )
    return tuple(out[None] for out in outs)


def solution(mesh):
    rows = P("dp", "ctx", None)
    in_specs = (rows, rows, rows, P(("ctx", "dp"), None), rows, rows, rows)
    return jax.shard_map(
        per_device, mesh=mesh, in_specs=in_specs, out_specs=(rows,) * 4, check_vma=False
    )
```

```python
import functools
import math

import jax
import jax.numpy as jnp
from jax import lax
from jax.experimental import pallas as pl
from jax.experimental.pallas import tpu as pltpu
from jax.sharding import PartitionSpec as P

HEADS = 16
HEAD = 128
TOK = 384
D = 4096
HD = HEADS * HEAD
GROUPS = 8
GCOLS = 256
N_CTX = 32
ROWS = 32
FIRST = 12
CHUNK = 512
AHEAD = 3
LAGS = (0, 3, 5, 6)
MEMORY_STEP = 9
QUERY_STEP = 2
MESH = pl.DeviceIdType.MESH
ORDERS = ((0, 1, 2), (1, 2, 0), (2, 0, 1))
BF16 = jnp.bfloat16
F32 = jnp.float32
NT = (((1,), (1,)), ((), ()))
TN = (((0,), (0,)), ((), ()))


def place():
    ctx = lax.axis_index("ctx")
    dp = lax.axis_index("dp")
    x = lax.rem(ctx, 4)
    y = lax.rem(ctx // 4, 4)
    z = (dp // 2) * 2 + ctx // 16
    return (x, y, z), lax.rem(dp, 2)


def device_of(at, core):
    x, y, z = at
    return (lax.rem(z, 2) * 16 + y * 4 + x, (z // 2) * 2 + core)


def moved(at, axis, by):
    out = list(at)
    out[axis] = lax.rem(out[axis] + by, 4)
    return tuple(out)


def view(buf, group, at, core, whole, half=None):
    picks = []
    for axis in range(2):
        if half is not None and half[0] == axis:
            picks.append(pl.ds(2 * half[1], 2))
        elif axis in whole:
            picks.append(slice(None))
        else:
            picks.append(at[axis])
    low = slice(None) if 2 in whole else lax.rem(at[2], 2)
    high = slice(None) if 2 in whole else at[2] // 2
    return buf.at[group, low, picks[1], picks[0], high, core]


def dot(a, b, dims=(((1,), (0,)), ((), ()))):
    return lax.dot_general(a, b, dims, preferred_element_type=F32)


def layer_kernel(
    factor,
    tok_hbm,
    key_hbm,
    val_hbm,
    w_hbm,
    qsp_hbm,
    ksp_hbm,
    cot_hbm,
    att,
    gtok,
    gkey,
    gval,
    wbuf,
    tok,
    keys,
    val,
    cot,
    qsp,
    ksp,
    mg,
    kgrad,
    vgrad,
    qgrad,
    projected,
    queries,
    local,
    m_send,
    m_in,
    m_out,
    m_state,
    a_send,
    a_in,
    a_out,
    a_state,
    own_sem,
    load_sem,
    send_sem,
    recv_sem,
    sib_sem,
    scan_sem,
):
    at, core = place()
    ctx = lax.axis_index("ctx")
    dp = lax.axis_index("dp")
    other_core = device_of(at, 1 - core)

    own = []
    for g in range(GROUPS):
        copy = pltpu.make_async_copy(
            w_hbm.at[:, pl.ds(g * GCOLS, GCOLS)], view(wbuf, g, at, core, ()), own_sem.at[g]
        )
        copy.start()
        own.append(copy)

    loads = []
    for number, (src, dst) in enumerate(
        (
            (key_hbm, keys),
            (ksp_hbm, ksp),
            (val_hbm, val),
            (cot_hbm, cot),
            (tok_hbm, tok),
            (qsp_hbm, qsp),
        )
    ):
        copy = pltpu.make_async_copy(src, dst, load_sem.at[number])
        copy.start()
        loads.append(copy)

    barrier = pltpu.get_barrier_semaphore()

    def greet(step, carry):
        pl.semaphore_signal(
            barrier, 1, device_id=(lax.rem(ctx + step, N_CTX), dp), device_id_type=MESH
        )
        return carry

    lax.fori_loop(1, N_CTX, greet, 0)
    far_z = 1 - at[2] // 2
    for low in (0, 1):
        pl.semaphore_signal(
            barrier,
            1,
            device_id=(low * 16 + at[1] * 4 + at[0], far_z * 2 + core),
            device_id_type=MESH,
        )
    pl.semaphore_signal(barrier, 1, device_id=other_core, device_id_type=MESH)
    pl.semaphore_wait(barrier, N_CTX + 2)

    def remote(part, sems, target):
        return pltpu.make_async_remote_copy(
            src_ref=part,
            dst_ref=part,
            send_sem=sems[0],
            recv_sem=sems[1],
            device_id=target,
            device_id_type=MESH,
        )

    def link(part, g, slot, target):
        return remote(part, (send_sem.at[g, slot], recv_sem.at[g, slot]), target)

    def spread(g, order, number):
        part = view(wbuf, g, at, core, order[:number])
        return [
            link(part, g, 3 * number + by - 1, device_of(moved(at, order[number], by), core))
            for by in (1, 3, 2)
        ]

    def near(g, order):
        part = view(wbuf, g, at, core, order[:2])
        return [
            link(part, g, 5 + way, device_of(moved(at, order[2], by), core))
            for way, by in ((1, 1), (2, 3))
        ]

    def far(g, order):
        left, right = moved(at, order[2], 3), moved(at, order[2], 1)
        split = 0 if order[2] == 1 else 1
        return [
            link(view(wbuf, g, here, core, order[:2], (split, half)), g, 8 + half, device_of(to, core))
            for half, here, to in ((0, left, right), (1, right, left))
        ]

    def sibling(g, order):
        return [
            remote(
                view(wbuf, g, moved(at, order[2], by), core, order[:2]),
                (sib_sem.at[0, g, by], sib_sem.at[1, g, by]),
                other_core,
            )
            for by in range(4)
        ]

    def ordered(g, act):
        for number, order in enumerate(ORDERS):

            @pl.when(lax.rem(g + core, 3) == number)
            def _(order=order):
                act(g, order)

    def start(copies):
        for copy in copies:
            copy.start()

    def first(g, order):
        start(spread(g, order, 0))

    def second(g, order):
        for copy in spread(g, order, 0):
            copy.wait_recv()
        start(spread(g, order, 1))

    def third(g, order):
        for copy in spread(g, order, 1):
            copy.wait_recv()
        start(near(g, order))
        sibling(g, order)[0].start()

    def fourth(g, order):
        arriving, onward, across = near(g, order), far(g, order), sibling(g, order)
        for half, by in ((0, 3), (1, 1)):
            arriving[half].wait_recv()
            onward[half].start()
            across[by].start()

    def fifth(g, order):
        for copy in far(g, order):
            copy.wait_recv()
        sibling(g, order)[2].start()

    def arrived(g, order):
        for copy in sibling(g, order):
            copy.wait_recv()

    def sent(g, order):
        for copy in (
            *spread(g, order, 0),
            *spread(g, order, 1),
            *near(g, order),
            *far(g, order),
            *sibling(g, order),
        ):
            copy.wait_send()

    def exchange(src, dst, number, tiles, base=0):
        def one(step, carry):
            other = lax.rem(ctx + step, N_CTX)
            pltpu.make_async_remote_copy(
                src_ref=src.at[pl.ds(base + other * tiles, tiles)],
                dst_ref=dst.at[pl.ds(base + ctx * tiles, tiles)],
                send_sem=scan_sem.at[0, number],
                recv_sem=scan_sem.at[1, number],
                device_id=(other, dp),
                device_id_type=MESH,
            ).start()
            return carry

        lax.fori_loop(1, N_CTX, one, 0)
        mine = pl.ds(base + ctx * tiles, tiles)
        dst[mine] = src[mine]

    def exchanged(src, dst, number, tiles, base=0):
        most = pl.ds(base, (N_CTX - 1) * tiles)
        pltpu.make_async_copy(src.at[most], dst.at[most], scan_sem.at[1, number]).wait()
        pltpu.make_async_copy(src.at[most], dst.at[most], scan_sem.at[0, number]).wait()

    def prefix(inbox, outbox, tiles, reverse, base=0):
        def add(step, total):
            source = N_CTX - 1 - step if reverse else step
            piece = pl.ds(base + source * tiles, tiles)
            outbox[piece] = total.astype(BF16)
            return total + inbox[piece].astype(F32)

        lax.fori_loop(0, N_CTX, add, jnp.zeros((tiles, 16, HEAD), F32))

    def columns(head):
        return pl.ds(pl.multiple_of(head * HEAD, HEAD), HEAD)

    def keep(product, first_row, first_col, below):
        rows = lax.broadcasted_iota(jnp.int32, product.shape, 0) + first_row
        cols = lax.broadcasted_iota(jnp.int32, product.shape, 1) + first_col
        return jnp.where(rows >= cols if below else rows <= cols, product, 0.0).astype(BF16)

    def below(a, b, c):
        wide = dot(keep(dot(a, b[:256], NT), 0, 0, True), c[:256])
        last = dot(keep(dot(a[256:], b[256:], NT), 0, 0, True), c[256:])
        return jnp.concatenate([wide[:256], wide[256:] + last], axis=0)

    def above(a, b, c):
        wide = dot(keep(dot(a, b[128:], NT), 0, 128, False), c[128:])
        head = dot(keep(dot(a[:128], b[:128], NT), 0, 0, False), c[:128])
        return jnp.concatenate([wide[:128] + head, wide[128:]], axis=0)

    def own_memory(head, carry):
        cols = columns(head)
        k = (keys[:, cols].astype(F32) * ksp[:, cols].astype(F32)).astype(BF16)
        keys[:, cols] = k
        state = dot(k, val[:, cols], TN).astype(BF16)
        m_send[pl.ds(head * 8, 8)] = state.reshape(8, 16, HEAD)
        return carry

    def own_query_grad(head, carry):
        cols = columns(head)
        qgrad[:, cols] = below(cot[:, cols], val[:, cols], keys[:, cols])
        return carry

    def use_memory(head, carry):
        cols = columns(head)
        state = m_state[pl.ds(head * 8, 8)].reshape(HEAD, HEAD)
        whole = qgrad[:, cols] + dot(cot[:, cols], state, NT)
        mg[:, cols] = (factor * whole * qsp[:, cols].astype(F32)).astype(BF16)
        att[:, cols] = (factor * (local[:, cols] + dot(queries[:, cols], state))).astype(BF16)
        return carry

    def project(g):
        projected[...] = dot(tok[...], wbuf[g].reshape(D, GCOLS))

    def attend(g):
        for one in range(2):
            head = 2 * g + one
            cols = columns(head)
            q = projected[:, one * HEAD : (one + 1) * HEAD] * qsp[:, cols].astype(F32)
            q = q.astype(BF16)
            queries[:, cols] = q
            k, v, c = keys[:, cols], val[:, cols], cot[:, cols]
            state = dot(q, c, TN).astype(BF16).reshape(8, 16, HEAD)
            a_send[pl.ds(head * 8, 8)] = state
            local[:, cols] = below(q, k, v)
            vgrad[:, cols] = above(k, q, c)
            kgrad[:, cols] = above(v, c, q)

    def token_grad(number, carry):
        pieces = [
            wbuf[g, number // 4, lax.rem(number, 4)].reshape(CHUNK, GCOLS) for g in range(GROUPS)
        ]
        total = dot(mg[...], jnp.concatenate(pieces, axis=1), NT)
        cols = pl.ds(pl.multiple_of(number * CHUNK, CHUNK), CHUNK)
        gtok[:, cols] = total.astype(BF16)
        return carry

    def finish(head, carry):
        cols = columns(head)
        state = a_state[pl.ds(head * 8, 8)].reshape(HEAD, HEAD)
        key_grad = kgrad[:, cols] + dot(val[:, cols], state, NT)
        gkey[:, cols] = (factor * key_grad * ksp[:, cols].astype(F32)).astype(BF16)
        value_grad = vgrad[:, cols] + dot(keys[:, cols], state)
        gval[:, cols] = (factor * value_grad).astype(BF16)
        return carry

    m_tiles, a_tiles, b_tiles = HEADS // 4, FIRST // 4, (HEADS - FIRST) // 4
    b_base = FIRST * 8
    for copy in own:
        copy.wait()

    def begin(g, carry):
        ordered(g, first)
        return carry

    lax.fori_loop(0, GROUPS, begin, 0)

    def ahead(g, carry):
        ordered(g, second)
        return carry

    lax.fori_loop(0, AHEAD, ahead, 0)
    for number in range(4):
        loads[number].wait()
    lax.fori_loop(0, HEADS, own_memory, 0, unroll=2)
    exchange(m_send, m_in, 0, m_tiles)

    def body(step, carry):
        for lag, act in zip((-AHEAD, *LAGS), (second, third, fourth, fifth, arrived)):
            low = max(lag, 0)

            @pl.when((step >= low) & (step < lag + GROUPS))
            def _(lag=lag, act=act):
                ordered(step - lag, act)

        last = LAGS[3]

        @pl.when((step >= QUERY_STEP) & (step < QUERY_STEP + 4))
        def _():
            for pair in range(2):
                for one in range(2):
                    own_query_grad(4 * (step - QUERY_STEP) + 2 * pair + one, 0)

        @pl.when(step == MEMORY_STEP)
        def _():
            exchanged(m_send, m_in, 0, m_tiles)
            prefix(m_in, m_out, m_tiles, False)
            exchange(m_out, m_state, 1, m_tiles)

        @pl.when(step == last)
        def _():
            loads[4].wait()
            loads[5].wait()

        @pl.when(step >= last)
        def _():
            project(step - last)

        @pl.when((step >= last) & (step >= 0))
        def _():
            attend(step - last)

        @pl.when(2 * (step - last + 1) == FIRST)
        def _():
            exchange(a_send, a_in, 2, a_tiles)

        return carry

    lax.fori_loop(0, GROUPS + LAGS[3], body, 0)
    exchange(a_send, a_in, 4, b_tiles, b_base)
    exchanged(a_send, a_in, 2, a_tiles)
    prefix(a_in, a_out, a_tiles, True)
    exchange(a_out, a_state, 3, a_tiles)
    exchanged(m_out, m_state, 1, m_tiles)
    lax.fori_loop(0, HEADS, use_memory, 0, unroll=2)
    exchanged(a_send, a_in, 4, b_tiles, b_base)
    prefix(a_in, a_out, b_tiles, True, b_base)
    exchange(a_out, a_state, 5, b_tiles, b_base)
    lax.fori_loop(0, 8, token_grad, 0)
    exchanged(a_out, a_state, 3, a_tiles)
    lax.fori_loop(0, FIRST, finish, 0, unroll=2)
    exchanged(a_out, a_state, 5, b_tiles, b_base)
    lax.fori_loop(FIRST, HEADS, finish, 0, unroll=2)

    def end(g, carry):
        ordered(g, sent)
        return carry

    lax.fori_loop(0, GROUPS, end, 0)


def scan_buffers(heads):
    return [pltpu.VMEM((heads * 8, 16, HEAD), BF16)] * 4


def layer(factor, tokens, key_input, values, q_weight, q_spikes, k_spikes, cotangent):
    wide = pltpu.VMEM((TOK, HD), BF16)
    wide_float = pltpu.VMEM((TOK, HD), F32)
    wide_int = pltpu.VMEM((TOK, HD), jnp.int32)
    anywhere = pl.BlockSpec(memory_space=pl.ANY)
    return pl.pallas_call(
        functools.partial(layer_kernel, factor),
        out_shape=(wide, pltpu.VMEM((TOK, D), BF16), wide, wide),
        in_specs=[anywhere] * 7,
        out_specs=(pl.BlockSpec(memory_space=pltpu.VMEM),) * 4,
        scratch_shapes=[
            pltpu.VMEM((GROUPS, 2, 4, 4, 2, 2, ROWS, GCOLS), BF16),
            pltpu.VMEM((TOK, D), BF16),
            wide,
            wide,
            wide,
            wide_int,
            wide_int,
            wide,
            wide_float,
            wide_float,
            wide_float,
            pltpu.VMEM((TOK, GCOLS), F32),
            wide,
            wide_float,
            *scan_buffers(HEADS),
            *scan_buffers(HEADS),
            pltpu.SemaphoreType.DMA((GROUPS,)),
            pltpu.SemaphoreType.DMA((6,)),
            pltpu.SemaphoreType.DMA((GROUPS, 10)),
            pltpu.SemaphoreType.DMA((GROUPS, 10)),
            pltpu.SemaphoreType.DMA((2, GROUPS, 4)),
            pltpu.SemaphoreType.DMA((2, 6)),
        ],
        compiler_params=pltpu.CompilerParams(
            collective_id=0, has_side_effects=True, vmem_limit_bytes=54 << 20
        ),
    )(tokens, key_input, values, q_weight, q_spikes, k_spikes, cotangent)


def write_kernel(*refs):
    sources, targets, sems = refs[:4], refs[4:8], refs[8]
    copies = [
        pltpu.make_async_copy(src, dst, sems.at[number])
        for number, (src, dst) in enumerate(zip(sources, targets))
    ]
    for copy in copies:
        copy.start()
    for copy in copies:
        copy.wait()


def write(arrays):
    return pl.pallas_call(
        write_kernel,
        out_shape=[jax.ShapeDtypeStruct(array.shape, array.dtype) for array in arrays],
        in_specs=[pl.BlockSpec(memory_space=pltpu.VMEM)] * 4,
        out_specs=[pl.BlockSpec(memory_space=pl.ANY)] * 4,
        scratch_shapes=[pltpu.SemaphoreType.DMA((4,))],
        compiler_params=pltpu.CompilerParams(vmem_limit_bytes=1 << 20),
    )(*arrays)


def per_device(tokens, key_input, values, q_weight, q_spikes, k_spikes, cotangent):
    sequence = tokens.shape[1] * lax.axis_size("ctx")
    factor = 3.0 / math.sqrt(HEAD * sequence)
    outs = layer(
        factor, tokens[0], key_input[0], values[0], q_weight, q_spikes[0], k_spikes[0], cotangent[0]
    )
    return tuple(out[None] for out in write(outs))


def solution(mesh):
    rows = P("dp", "ctx", None)
    in_specs = (rows, rows, rows, P(("ctx", "dp"), None), rows, rows, rows)
    return jax.shard_map(
        per_device, mesh=mesh, in_specs=in_specs, out_specs=(rows,) * 4, check_vma=False
    )
```

```python
import functools
import math

import jax
import jax.numpy as jnp
from jax import lax
from jax.experimental import pallas as pl
from jax.experimental.pallas import tpu as pltpu
from jax.sharding import PartitionSpec as P

HEADS = 16
HEAD = 128
TOK = 384
D = 4096
HD = HEADS * HEAD
GROUPS = 8
GCOLS = 256
N_CTX = 32
ROWS = 32
FIRST = 12
CHUNK = 512
STRIP = 96
AHEAD = 3
LAGS = (0, 3, 5, 6)
MEMORY_STEP = 9
QUERY_STEP = 2
MESH = pl.DeviceIdType.MESH
ORDERS = ((0, 1, 2), (1, 2, 0), (2, 0, 1))
BF16 = jnp.bfloat16
F32 = jnp.float32
NT = (((1,), (1,)), ((), ()))
TN = (((0,), (0,)), ((), ()))


def place():
    ctx = lax.axis_index("ctx")
    dp = lax.axis_index("dp")
    x = lax.rem(ctx, 4)
    y = lax.rem(ctx // 4, 4)
    z = (dp // 2) * 2 + ctx // 16
    return (x, y, z), lax.rem(dp, 2)


def device_of(at, core):
    x, y, z = at
    return (lax.rem(z, 2) * 16 + y * 4 + x, (z // 2) * 2 + core)


def moved(at, axis, by):
    out = list(at)
    out[axis] = lax.rem(out[axis] + by, 4)
    return tuple(out)


def view(buf, group, at, core, whole, half=None):
    picks = []
    for axis in range(2):
        if half is not None and half[0] == axis:
            picks.append(pl.ds(2 * half[1], 2))
        elif axis in whole:
            picks.append(slice(None))
        else:
            picks.append(at[axis])
    low = slice(None) if 2 in whole else lax.rem(at[2], 2)
    high = slice(None) if 2 in whole else at[2] // 2
    return buf.at[group, low, picks[1], picks[0], high, core]


def dot(a, b, dims=(((1,), (0,)), ((), ()))):
    return lax.dot_general(a, b, dims, preferred_element_type=F32)


def layer_kernel(
    factor,
    tok_hbm,
    key_hbm,
    val_hbm,
    w_hbm,
    qsp_hbm,
    ksp_hbm,
    cot_hbm,
    att,
    gtok,
    gkey,
    gval,
    wbuf,
    tok,
    keys,
    val,
    cot,
    qsp,
    ksp,
    mg,
    kgrad,
    vgrad,
    qgrad,
    projected,
    queries,
    local,
    m_send,
    m_in,
    m_out,
    m_state,
    a_send,
    a_in,
    a_out,
    a_state,
    own_sem,
    load_sem,
    send_sem,
    recv_sem,
    sib_sem,
    scan_sem,
):
    at, core = place()
    ctx = lax.axis_index("ctx")
    dp = lax.axis_index("dp")
    other_core = device_of(at, 1 - core)

    own = []
    for g in range(GROUPS):
        copy = pltpu.make_async_copy(
            w_hbm.at[:, pl.ds(g * GCOLS, GCOLS)], view(wbuf, g, at, core, ()), own_sem.at[g]
        )
        copy.start()
        own.append(copy)

    loads = []
    for number, (src, dst) in enumerate(
        (
            (key_hbm, keys),
            (ksp_hbm, ksp),
            (val_hbm, val),
            (cot_hbm, cot),
            (tok_hbm, tok),
            (qsp_hbm, qsp),
        )
    ):
        loads.append(pltpu.make_async_copy(src, dst, load_sem.at[number]))
    for copy in loads[:3]:
        copy.start()

    barrier = pltpu.get_barrier_semaphore()

    def greet(step, carry):
        pl.semaphore_signal(
            barrier, 1, device_id=(lax.rem(ctx + step, N_CTX), dp), device_id_type=MESH
        )
        return carry

    lax.fori_loop(1, N_CTX, greet, 0)
    far_z = 1 - at[2] // 2
    for low in (0, 1):
        pl.semaphore_signal(
            barrier,
            1,
            device_id=(low * 16 + at[1] * 4 + at[0], far_z * 2 + core),
            device_id_type=MESH,
        )
    pl.semaphore_signal(barrier, 1, device_id=other_core, device_id_type=MESH)
    pl.semaphore_wait(barrier, N_CTX + 2)

    def remote(part, sems, target):
        return pltpu.make_async_remote_copy(
            src_ref=part,
            dst_ref=part,
            send_sem=sems[0],
            recv_sem=sems[1],
            device_id=target,
            device_id_type=MESH,
        )

    def link(part, g, slot, target):
        return remote(part, (send_sem.at[g, slot], recv_sem.at[g, slot]), target)

    def spread(g, order, number):
        part = view(wbuf, g, at, core, order[:number])
        return [
            link(part, g, 3 * number + by - 1, device_of(moved(at, order[number], by), core))
            for by in (1, 3, 2)
        ]

    def near(g, order):
        part = view(wbuf, g, at, core, order[:2])
        return [
            link(part, g, 5 + way, device_of(moved(at, order[2], by), core))
            for way, by in ((1, 1), (2, 3))
        ]

    def far(g, order):
        left, right = moved(at, order[2], 3), moved(at, order[2], 1)
        split = 0 if order[2] == 1 else 1
        return [
            link(view(wbuf, g, here, core, order[:2], (split, half)), g, 8 + half, device_of(to, core))
            for half, here, to in ((0, left, right), (1, right, left))
        ]

    def sibling(g, order):
        return [
            remote(
                view(wbuf, g, moved(at, order[2], by), core, order[:2]),
                (sib_sem.at[0, g, by], sib_sem.at[1, g, by]),
                other_core,
            )
            for by in range(4)
        ]

    def ordered(g, act):
        for number, order in enumerate(ORDERS):

            @pl.when(lax.rem(g + core, 3) == number)
            def _(order=order):
                act(g, order)

    def start(copies):
        for copy in copies:
            copy.start()

    def first(g, order):
        start(spread(g, order, 0))

    def second(g, order):
        for copy in spread(g, order, 0):
            copy.wait_recv()
        start(spread(g, order, 1))

    def third(g, order):
        for copy in spread(g, order, 1):
            copy.wait_recv()
        start(near(g, order))
        sibling(g, order)[0].start()

    def fourth(g, order):
        arriving, onward, across = near(g, order), far(g, order), sibling(g, order)
        for half, by in ((0, 3), (1, 1)):
            arriving[half].wait_recv()
            onward[half].start()
            across[by].start()

    def fifth(g, order):
        for copy in far(g, order):
            copy.wait_recv()
        sibling(g, order)[2].start()

    def arrived(g, order):
        for copy in sibling(g, order):
            copy.wait_recv()

    def sent(g, order):
        for copy in (
            *spread(g, order, 0),
            *spread(g, order, 1),
            *near(g, order),
            *far(g, order),
            *sibling(g, order),
        ):
            copy.wait_send()

    def exchange(src, dst, number, tiles, base=0):
        def one(step, carry):
            other = lax.rem(ctx + step, N_CTX)
            pltpu.make_async_remote_copy(
                src_ref=src.at[pl.ds(base + other * tiles, tiles)],
                dst_ref=dst.at[pl.ds(base + ctx * tiles, tiles)],
                send_sem=scan_sem.at[0, number],
                recv_sem=scan_sem.at[1, number],
                device_id=(other, dp),
                device_id_type=MESH,
            ).start()
            return carry

        lax.fori_loop(1, N_CTX, one, 0)
        mine = pl.ds(base + ctx * tiles, tiles)
        dst[mine] = src[mine]

    def exchanged(src, dst, number, tiles, base=0):
        most = pl.ds(base, (N_CTX - 1) * tiles)
        pltpu.make_async_copy(src.at[most], dst.at[most], scan_sem.at[1, number]).wait()
        pltpu.make_async_copy(src.at[most], dst.at[most], scan_sem.at[0, number]).wait()

    def prefix(inbox, outbox, tiles, reverse, base=0):
        def add(step, total):
            source = N_CTX - 1 - step if reverse else step
            piece = pl.ds(base + source * tiles, tiles)
            outbox[piece] = total.astype(BF16)
            return total + inbox[piece].astype(F32)

        lax.fori_loop(0, N_CTX, add, jnp.zeros((tiles, 16, HEAD), F32))

    def columns(head):
        return pl.ds(pl.multiple_of(head * HEAD, HEAD), HEAD)

    def keep(product, first_row, first_col, below):
        rows = lax.broadcasted_iota(jnp.int32, product.shape, 0) + first_row
        cols = lax.broadcasted_iota(jnp.int32, product.shape, 1) + first_col
        return jnp.where(rows >= cols if below else rows <= cols, product, 0.0).astype(BF16)

    def below(a, b, c):
        wide = dot(keep(dot(a, b[:256], NT), 0, 0, True), c[:256])
        last = dot(keep(dot(a[256:], b[256:], NT), 0, 0, True), c[256:])
        return jnp.concatenate([wide[:256], wide[256:] + last], axis=0)

    def above(a, b, c):
        wide = dot(keep(dot(a, b[128:], NT), 0, 128, False), c[128:])
        head = dot(keep(dot(a[:128], b[:128], NT), 0, 0, False), c[:128])
        return jnp.concatenate([wide[:128] + head, wide[128:]], axis=0)

    def own_memory(head, carry):
        cols = columns(head)
        k = (keys[:, cols].astype(F32) * ksp[:, cols].astype(F32)).astype(BF16)
        keys[:, cols] = k
        state = dot(k, val[:, cols], TN).astype(BF16)
        m_send[pl.ds(head * 8, 8)] = state.reshape(8, 16, HEAD)
        return carry

    def own_query_grad(head, carry):
        cols = columns(head)
        qgrad[:, cols] = below(cot[:, cols], val[:, cols], keys[:, cols])
        return carry

    def use_memory(head, carry):
        cols = columns(head)
        state = m_state[pl.ds(head * 8, 8)].reshape(HEAD, HEAD)
        whole = qgrad[:, cols] + dot(cot[:, cols], state, NT)
        mg[:, cols] = (factor * whole * qsp[:, cols].astype(F32)).astype(BF16)
        att[:, cols] = (factor * (local[:, cols] + dot(queries[:, cols], state))).astype(BF16)
        return carry

    def project(g):
        projected[...] = dot(tok[...], wbuf[g].reshape(D, GCOLS))

    def attend(g):
        for one in range(2):
            head = 2 * g + one
            cols = columns(head)
            q = projected[:, one * HEAD : (one + 1) * HEAD] * qsp[:, cols].astype(F32)
            q = q.astype(BF16)
            queries[:, cols] = q
            k, v, c = keys[:, cols], val[:, cols], cot[:, cols]
            state = dot(q, c, TN).astype(BF16).reshape(8, 16, HEAD)
            a_send[pl.ds(head * 8, 8)] = state
            local[:, cols] = below(q, k, v)
            vgrad[:, cols] = above(k, q, c)
            kgrad[:, cols] = above(v, c, q)

    def token_grad(number, carry):
        pieces = [
            wbuf[g, number // 4, lax.rem(number, 4)].reshape(CHUNK, GCOLS) for g in range(GROUPS)
        ]
        total = dot(mg[...], jnp.concatenate(pieces, axis=1), NT)
        cols = pl.ds(pl.multiple_of(number * CHUNK, CHUNK), CHUNK)
        gtok[:, cols] = total.astype(BF16)
        return carry

    def finish(head, carry):
        cols = columns(head)
        state = a_state[pl.ds(head * 8, 8)].reshape(HEAD, HEAD)
        key_grad = kgrad[:, cols] + dot(val[:, cols], state, NT)
        gkey[:, cols] = (factor * key_grad * ksp[:, cols].astype(F32)).astype(BF16)
        value_grad = vgrad[:, cols] + dot(keys[:, cols], state)
        gval[:, cols] = (factor * value_grad).astype(BF16)
        return carry

    m_tiles, a_tiles, b_tiles = HEADS // 4, FIRST // 4, (HEADS - FIRST) // 4
    b_base = FIRST * 8
    for copy in own:
        copy.wait()

    def begin(g, carry):
        ordered(g, first)
        return carry

    lax.fori_loop(0, GROUPS, begin, 0)

    def ahead(g, carry):
        ordered(g, second)
        return carry

    lax.fori_loop(0, AHEAD, ahead, 0)
    for copy in loads[:3]:
        copy.wait()
    for copy in loads[3:]:
        copy.start()
    lax.fori_loop(0, HEADS, own_memory, 0, unroll=2)
    exchange(m_send, m_in, 0, m_tiles)
    loads[3].wait()

    def body(step, carry):
        for lag, act in zip((-AHEAD, *LAGS), (second, third, fourth, fifth, arrived)):
            low = max(lag, 0)

            @pl.when((step >= low) & (step < lag + GROUPS))
            def _(lag=lag, act=act):
                ordered(step - lag, act)

        last = LAGS[3]

        @pl.when((step >= QUERY_STEP) & (step < QUERY_STEP + 4))
        def _():
            for pair in range(2):
                for one in range(2):
                    own_query_grad(4 * (step - QUERY_STEP) + 2 * pair + one, 0)

        @pl.when(step == MEMORY_STEP)
        def _():
            exchanged(m_send, m_in, 0, m_tiles)
            prefix(m_in, m_out, m_tiles, False)
            exchange(m_out, m_state, 1, m_tiles)

        @pl.when(step == last)
        def _():
            loads[4].wait()
            loads[5].wait()

        @pl.when(step >= last)
        def _():
            project(step - last)

        @pl.when((step >= last) & (step >= 0))
        def _():
            attend(step - last)

        @pl.when(2 * (step - last + 1) == FIRST)
        def _():
            exchange(a_send, a_in, 2, a_tiles)

        return carry

    lax.fori_loop(0, GROUPS + LAGS[3], body, 0)
    exchange(a_send, a_in, 4, b_tiles, b_base)
    exchanged(a_send, a_in, 2, a_tiles)
    prefix(a_in, a_out, a_tiles, True)
    exchange(a_out, a_state, 3, a_tiles)
    exchanged(m_out, m_state, 1, m_tiles)
    lax.fori_loop(0, HEADS, use_memory, 0, unroll=2)
    exchanged(a_send, a_in, 4, b_tiles, b_base)
    prefix(a_in, a_out, b_tiles, True, b_base)
    exchange(a_out, a_state, 5, b_tiles, b_base)
    lax.fori_loop(0, 8, token_grad, 0)
    exchanged(a_out, a_state, 3, a_tiles)
    lax.fori_loop(0, FIRST, finish, 0, unroll=2)
    exchanged(a_out, a_state, 5, b_tiles, b_base)
    lax.fori_loop(FIRST, HEADS, finish, 0, unroll=2)

    def end(g, carry):
        ordered(g, sent)
        return carry

    lax.fori_loop(0, GROUPS, end, 0)


def scan_buffers(heads):
    return [pltpu.VMEM((heads * 8, 16, HEAD), BF16)] * 4


def layer(factor, tokens, key_input, values, q_weight, q_spikes, k_spikes, cotangent):
    wide = pltpu.VMEM((TOK, HD), BF16)
    wide_float = pltpu.VMEM((TOK, HD), F32)
    wide_int = pltpu.VMEM((TOK, HD), jnp.int32)
    anywhere = pl.BlockSpec(memory_space=pl.ANY)
    return pl.pallas_call(
        functools.partial(layer_kernel, factor),
        out_shape=(wide, pltpu.VMEM((TOK, D), BF16), wide, wide),
        in_specs=[anywhere] * 7,
        out_specs=(pl.BlockSpec(memory_space=pltpu.VMEM),) * 4,
        scratch_shapes=[
            pltpu.VMEM((GROUPS, 2, 4, 4, 2, 2, ROWS, GCOLS), BF16),
            pltpu.VMEM((TOK, D), BF16),
            wide,
            wide,
            wide,
            wide_int,
            wide_int,
            wide,
            wide_float,
            wide_float,
            wide_float,
            pltpu.VMEM((TOK, GCOLS), F32),
            wide,
            wide_float,
            *scan_buffers(HEADS),
            *scan_buffers(HEADS),
            pltpu.SemaphoreType.DMA((GROUPS,)),
            pltpu.SemaphoreType.DMA((6,)),
            pltpu.SemaphoreType.DMA((GROUPS, 10)),
            pltpu.SemaphoreType.DMA((GROUPS, 10)),
            pltpu.SemaphoreType.DMA((2, GROUPS, 4)),
            pltpu.SemaphoreType.DMA((2, 6)),
        ],
        compiler_params=pltpu.CompilerParams(
            collective_id=0, has_side_effects=True, vmem_limit_bytes=54 << 20
        ),
    )(tokens, key_input, values, q_weight, q_spikes, k_spikes, cotangent)


def write_kernel(*refs):
    sources, targets, sems = refs[:4], refs[4:8], refs[8]
    copies = [
        pltpu.make_async_copy(
            src.at[pl.ds(part * STRIP, STRIP)], dst.at[pl.ds(part * STRIP, STRIP)], sems.at[number, part]
        )
        for number, (src, dst) in enumerate(zip(sources, targets))
        for part in range(TOK // STRIP)
    ]
    for copy in copies:
        copy.start()
    for copy in copies:
        copy.wait()


def write(arrays):
    return pl.pallas_call(
        write_kernel,
        out_shape=[jax.ShapeDtypeStruct(array.shape, array.dtype) for array in arrays],
        in_specs=[pl.BlockSpec(memory_space=pltpu.VMEM)] * 4,
        out_specs=[pl.BlockSpec(memory_space=pl.ANY)] * 4,
        scratch_shapes=[pltpu.SemaphoreType.DMA((4, TOK // STRIP))],
        compiler_params=pltpu.CompilerParams(vmem_limit_bytes=1 << 20),
    )(*arrays)


def per_device(tokens, key_input, values, q_weight, q_spikes, k_spikes, cotangent):
    sequence = tokens.shape[1] * lax.axis_size("ctx")
    factor = 3.0 / math.sqrt(HEAD * sequence)
    outs = layer(
        factor, tokens[0], key_input[0], values[0], q_weight, q_spikes[0], k_spikes[0], cotangent[0]
    )
    return tuple(out[None] for out in write(outs))


def solution(mesh):
    rows = P("dp", "ctx", None)
    in_specs = (rows, rows, rows, P(("ctx", "dp"), None), rows, rows, rows)
    return jax.shard_map(
        per_device, mesh=mesh, in_specs=in_specs, out_specs=(rows,) * 4, check_vma=False
    )
```
